256 devices in a mesh: tile: 64 (over y, x_hi, z), rcpt: 4 (over x_lo, core).
Axes of the slice: x: 4 (x_hi: 2, x_lo: 2; x = x_hi * 2 + x_lo), y: 4, z: 8, core: 2. Of those that a mesh axis runs over, the one named last changes fastest.
Arguments:
- adjoint_state: float32 [64, 16, 1024, 256], P('rcpt', None, 'tile'), may hold values from -6 to 6
- met_fields: bfloat16 [12, 3, 16, 1024, 256], P(None, None, 'rcpt', 'tile'), may hold values from -0.34960938 to 0.34960938
- forcing: bfloat16 [64, 1024, 256], P(None, 'tile'), may hold values from -6 to 6
- cluster_ids: int32 [64], P('rcpt'), may hold values from 0 to 63
- hour_index: int32 [2], replicated, may hold values from 0 to 11
Outputs:
- adjoint_out: float32 [64, 16, 1024, 256], P('rcpt', None, 'tile')
The draws below stay inside these ranges and needn't reach their ends.
All inputs are finite; a program needn't handle non-finite values.
Results may differ from the reference program's by a relative error of at most 0.00035.
Values may be sent and summed in bfloat16 or wider, within the bound.
No kernel may reach another device: no remote copies, remote signals or barrier semaphores. Data moves between devices by JAX's collectives and lax.ppermute only.
A program may use at most 64 MiB of HBM per device.

```python
import jax
import jax.numpy as jnp
from jax import lax

TRACERS = 64
CLUSTERS = 64
LEV = 16
LAT = 256
HOURS = 12
STEPS = 2
NLON = 1024


def place_ends(array, stream_key, smallest, largest):
    longest = array.shape.index(max(array.shape))
    spots = []
    for shift in (0, 1):
        where = [jax.random.randint(jax.random.fold_in(stream_key, axis), (), 0, length) for axis, length in enumerate(array.shape)]
        where[longest] = (where[longest] + shift) % array.shape[longest]
        spots.append(tuple(where))
    return array.at[spots[0]].set(smallest).at[spots[1]].set(largest)


def block_levels(rng, dims, pieces, low, largest):
    def one(dim, parts):
        draws = jax.random.uniform(jax.random.fold_in(jax.random.fold_in(rng, 6), dim), (parts,), jnp.float32, low / len(pieces), largest / len(pieces))
        return jnp.repeat(jnp.exp(draws), dims[dim] // parts).reshape((-1,) + (1,) * (len(dims) - dim - 1))

    level = one(*pieces[0])
    for cut in pieces[1:]:
        level = level * one(*cut)
    return level


def centred(key, shape, scale, bound, cuts=(), dtype=jnp.bfloat16):
    level = block_levels(key, shape, cuts, -0.22, 0.18) if cuts else 1.0
    drawn = jax.random.normal(key, shape, jnp.float32) * scale * level
    return jnp.minimum(jnp.maximum(drawn, -bound), bound).astype(dtype)


def setup_inputs(seed: int = 0) -> dict:
    arg_keys = jax.random.split(jax.random.key(seed), 6)
    adjoint_state = centred(arg_keys[0], (TRACERS, LEV, NLON, LAT), 1.0, 6.0, ((0, 4), (2, 64)), jnp.float32)
    met_fields = jnp.clip(jax.random.uniform(arg_keys[1], (HOURS, 3, LEV, NLON, LAT), jnp.float32, -0.34960938, 0.34960938) * block_levels(arg_keys[1], (HOURS, 3, LEV, NLON, LAT), ((2, 4), (3, 64)), -0.4, 0.0), -0.34960938, 0.34960938).astype(jnp.bfloat16)
    forcing = centred(arg_keys[2], (CLUSTERS, NLON, LAT), 1.0, 6.0, ((1, 64),))
    cluster_ids = place_ends(jax.random.randint(arg_keys[3], (TRACERS,), 0, CLUSTERS), jax.random.fold_in(arg_keys[3], 1), 0, CLUSTERS - 1).astype(jnp.int32)
    hour_index = jax.random.randint(arg_keys[4], (STEPS,), 0, HOURS).astype(jnp.int32)
    return dict(adjoint_state=adjoint_state, met_fields=met_fields, forcing=forcing, cluster_ids=cluster_ids, hour_index=hour_index)


def horizontal(lam, winds):
    cx = winds[0].astype(jnp.float32)
    cy = winds[1].astype(jnp.float32)
    px = lam * jnp.maximum(cx, 0.0)
    mx = lam * jnp.minimum(cx, 0.0)
    py = lam * jnp.maximum(cy, 0.0)
    my = lam * jnp.minimum(cy, 0.0)
    east = jnp.roll(px, -1, axis=2)
    west = jnp.roll(mx, 1, axis=2)
    zero = jnp.zeros_like(py[..., :1])
    north = jnp.concatenate([py[..., 1:], zero], axis=3)
    south = jnp.concatenate([zero, my[..., :-1]], axis=3)
    return lam * (1.0 - jnp.abs(cx) - jnp.abs(cy)) + east - west + north - south


def vertical(lam, mixing):
    coeff = 0.02 + 0.25 * jnp.abs(mixing.astype(jnp.float32))
    flux = coeff[:-1] * (lam[:, 1:] - lam[:, :-1])
    zero = jnp.zeros_like(flux[:, :1])
    return jnp.concatenate([flux, zero], axis=1) - jnp.concatenate([zero, flux], axis=1)


def reference(adjoint_state, met_fields, forcing, cluster_ids, hour_index):
    rows = forcing[cluster_ids].astype(jnp.float32)
    lam = adjoint_state
    for step in range(STEPS):
        metnow = lax.dynamic_index_in_dim(met_fields, hour_index[step], 0, keepdims=False)
        state = horizontal(lam, metnow) + vertical(lam, metnow[2])
        lam = state.at[:, -1].add(rows)
    return lam
```

```python
import functools

import jax
import jax.numpy as jnp
from jax import lax
from jax.experimental import pallas as pl
from jax.experimental.pallas import tpu as pltpu
from jax.sharding import PartitionSpec as P

BF = jnp.bfloat16
F32 = jnp.float32
SM = pl.BlockSpec(memory_space=pltpu.SMEM)
VM = pl.BlockSpec(memory_space=pltpu.VMEM)
HB = pl.BlockSpec(memory_space=pl.ANY)
LN = 128


def passed_along(block, axis, distance):
    n = lax.axis_size(axis)
    return lax.ppermute(block, axis, [((i - distance) % n, i) for i in range(n)])


def pick_kernel(hour, met, own, edge_w, edge_e, sem):
    copies = [pltpu.make_async_copy(met.at[hour[s]], own.at[s], sem.at[s]) for s in range(2)]
    for c in copies:
        c.start()
    for c in copies:
        c.wait()
    cols = own.shape[3]
    for out, near, far in ((edge_w, 0, 1), (edge_e, cols - 1, cols - 2)):
        for n, (s, f, c) in enumerate(((0, 0, near), (0, 1, near), (0, 2, near), (1, 0, near), (0, 0, far))):
            for k in range(own.shape[2]):
                out[n, k] = own[s, f, k].astype(F32)[c].astype(BF)


def pick(hour, met):
    _, f, k, i, j = met.shape
    return pl.pallas_call(
        pick_kernel,
        out_shape=[
            jax.ShapeDtypeStruct((2, f, k, i, j), BF),
            jax.ShapeDtypeStruct((5, k, j), BF),
            jax.ShapeDtypeStruct((5, k, j), BF),
        ],
        in_specs=[SM, HB],
        out_specs=[VM, VM, VM],
        scratch_shapes=[pltpu.SemaphoreType.DMA((2,))],
        name="pick",
    )(hour, met)


def pack_kernel(ids, lam, forcing, to_w, to_e, buf, rows, sem, rsem):
    nt, nk, ni, nj = lam.shape
    nb = nj // LN
    copies = []
    for b in range(nb):
        copies.append(
            pltpu.make_async_copy(lam.at[:, :, :, b * LN : (b + 1) * LN], buf.at[b], sem.at[b])
        )
        copies[-1].start()
    rcopies = [pltpu.make_async_copy(forcing.at[ids[t]], rows.at[t], rsem.at[t]) for t in range(nt)]
    for c in rcopies:
        c.start()
    for c in rcopies:
        c.wait()
    for t in range(nt):
        r = rows[t].astype(F32)
        to_w[2 * nt, t] = r[0].astype(BF)
        to_e[2 * nt, t] = r[ni - 1].astype(BF)
    for b in range(nb):
        copies[b].wait()
        flat = buf.at[b].reshape(nt * nk * ni, LN)
        for t in range(nt):
            for out, near, far in ((to_w, 0, 1), (to_e, ni - 1, ni - 2)):
                for n, c in enumerate((near, far)):
                    x = flat[pl.ds(t * nk * ni + c, nk, stride=ni), :]
                    out[n * nt + t, :, b * LN : (b + 1) * LN] = x.astype(BF)


def pack(ids, lam, forcing):
    nt, nk, ni, nj = lam.shape
    out = jax.ShapeDtypeStruct((2 * nt + 1, nk, nj), BF)
    return pl.pallas_call(
        pack_kernel,
        out_shape=[out, out],
        in_specs=[SM, HB, HB],
        out_specs=[VM, VM],
        scratch_shapes=[
            pltpu.VMEM((nj // LN, nt, nk, ni, LN), F32),
            pltpu.VMEM((nt, ni, nj), BF),
            pltpu.SemaphoreType.DMA((nj // LN,)),
            pltpu.SemaphoreType.DMA((nt,)),
        ],
        name="pack",
    )(ids, lam, forcing)


UP = 8


def main_kernel(ids, lam, met, edges, from_w, from_e, forcing, out,
                l0, l1, co, hs, hc, h1, rows, res, sem, rsem, osem):
    nt, nk, ni, nj = lam.shape
    nb = nj // LN
    nl = met.shape[3]
    lane = lax.broadcasted_iota(jnp.int32, (8, LN), 1)
    first, last = lane == 0, lane == LN - 1
    lane1 = lax.broadcasted_iota(jnp.int32, (ni, LN), 1)

    copies = [
        pltpu.make_async_copy(
            lam.at[:, :, :, b * LN : (b + 1) * LN], l0.at[b, :, :, UP : UP + ni, :], sem.at[b])
        for b in range(nb)
    ]
    for c in copies:
        c.start()
    rcopies = [pltpu.make_async_copy(forcing.at[ids[t]], rows.at[t], rsem.at[t]) for t in range(nt)]
    for c in rcopies:
        c.start()

    for side, src in ((0, from_e), (1, from_w)):
        for n in range(2):
            for t in range(nt):
                for b in range(nb):
                    hs[side + 2 * n, b, t] = src[n * nt + t, :, b * LN : (b + 1) * LN].astype(F32)

    def fill(field, s, k, b, x):
        co[s, field, b, k, UP : UP + ni, :] = x

    def coeffs(k, _):
        r = k // nl
        q = lax.rem(k, nl)
        kd = jnp.maximum(k - 1, 0)
        top = (k < nk - 1).astype(F32)
        bot = (k > 0).astype(F32)
        for s in range(2):
            for b in range(nb):
                sl = pl.ds(b * LN, LN)
                cx = met[r, s, 0, q, :, sl].astype(F32)
                cy = met[r, s, 1, q, :, sl].astype(F32)
                ku = (0.02 + 0.25 * jnp.abs(met[r, s, 2, q, :, sl].astype(F32))) * top
                km = (0.02 + 0.25 * jnp.abs(met[kd // nl, s, 2, lax.rem(kd, nl), :, sl].astype(F32))) * bot
                n = jnp.maximum(cy, 0.0)
                o = -jnp.minimum(cy, 0.0)
                if b == 0:
                    n = jnp.where(lane1 == 0, 0.0, n)
                if b == nb - 1:
                    o = jnp.where(lane1 == LN - 1, 0.0, o)
                fill(0, s, k, b, 1.0 - jnp.abs(cx) - jnp.abs(cy) - ku - km)
                fill(1, s, k, b, jnp.maximum(cx, 0.0))
                fill(2, s, k, b, -jnp.minimum(cx, 0.0))
                fill(3, s, k, b, n)
                fill(4, s, k, b, o)
                fill(5, s, k, b, ku)
                fill(6, s, k, b, km)
        return 0

    lax.fori_loop(0, nk, coeffs, 0)

    for side in range(2):
        for b in range(nb):
            sl = pl.ds(b * LN, LN)
            sg = 1.0 if side == 0 else -1.0

            def levels(n):
                return jnp.concatenate([edges[r, side, n, :, sl].astype(F32) for r in range(nk // nl)], axis=0)

            cx, cy, m, cx1, far = (levels(n) for n in range(5))
            lev = lax.broadcasted_iota(jnp.int32, (nk, LN), 0)
            kk = 0.02 + 0.25 * jnp.abs(m)
            ku = jnp.where(lev == nk - 1, 0.0, kk)
            km = jnp.where(lev == 0, 0.0, pltpu.roll(kk, 1, 0))
            n = jnp.maximum(cy, 0.0)
            o = -jnp.minimum(cy, 0.0)
            if b == 0:
                n = jnp.where(lev * 0 + lane1 == 0, 0.0, n)
            if b == nb - 1:
                o = jnp.where(lane1 == LN - 1, 0.0, o)
            hc[side, 0, b] = 1.0 - jnp.abs(cx) - jnp.abs(cy) - ku - km
            hc[side, 1, b] = jnp.maximum(sg * far, 0.0)
            hc[side, 3, b] = n
            hc[side, 4, b] = o
            hc[side, 5, b] = ku
            hc[side, 6, b] = km
            e0 = jnp.maximum(sg * cx, 0.0)
            e1 = jnp.maximum(sg * cx1, 0.0)
            row = UP + ni if side == 0 else UP - 1
            for s, e in ((0, e0), (1, e1)):
                for k in range(nk):
                    co[s, 1 + side, b, k, row : row + 1, :] = e[k : k + 1]

    for c in copies:
        c.wait()

    f0 = [l0.at[b].reshape(nt * nk * 32, LN) for b in range(nb)]
    f1 = [l1.at[b].reshape(nt * nk * 32, LN) for b in range(nb)]
    for b in range(nb):
        for side in range(2):
            own = UP + ni - 1 if side == 0 else UP
            row = UP + ni if side == 0 else UP - 1
            cf = co.at[0, 2 - side, b].reshape(nk * 32, LN)
            hc[side, 2, b] = cf[pl.ds(own, nk, stride=32), :]
            for t in range(nt):
                f0[b][pl.ds(t * nk * 32 + row, nk, stride=32), :] = hs[side, b, t]

    def roll2(x, sh):
        return pltpu.roll(x, sh % LN, 1)

    def shifted(p, o):
        rp = [roll2(x, -1) for x in p]
        ro = [roll2(x, 1) for x in o]
        north = [jnp.where(last, rp[(b + 1) % nb], rp[b]) for b in range(nb)]
        south = [jnp.where(first, ro[(b - 1) % nb], ro[b]) for b in range(nb)]
        return [north[b] + south[b] for b in range(nb)]

    for side in range(2):
        own = UP + ni - 1 if side == 0 else UP
        row = UP + ni if side == 0 else UP - 1
        for h in range(nk // 8):
            c = [[hc[side, f, b, h * 8 : h * 8 + 8, :] for b in range(nb)] for f in range(7)]

            def one(t, _):
                base = t * nk
                x = [hs[side, b, t, h * 8 : h * 8 + 8, :] for b in range(nb)]
                far = [hs[side + 2, b, t, h * 8 : h * 8 + 8, :] for b in range(nb)]
                mine = [f0[b][pl.ds((base + h * 8) * 32 + own, 8, stride=32), :] for b in range(nb)]
                ns = shifted([x[b] * c[3][b] for b in range(nb)], [x[b] * c[4][b] for b in range(nb)])
                for b in range(nb):
                    up = hs[side, b, t, pl.ds(min(h * 8 + 1, nk - 8), 8), :] if h * 8 + 9 <= nk else pltpu.roll(x[b], 7, 0)
                    dn = hs[side, b, t, pl.ds(h * 8 - 1, 8), :] if h else pltpu.roll(x[b], 1, 0)
                    y = (x[b] * c[0][b] + far[b] * c[1][b] + mine[b] * c[2][b] + ns[b]
                         + up * c[5][b] + dn * c[6][b])
                    h1[side, b, t, h * 8 : h * 8 + 8, :] = y
                return 0

            lax.fori_loop(0, nt, one, 0)
    for c in rcopies:
        c.wait()
    for side, src in ((0, from_e), (1, from_w)):
        row = UP + ni if side == 0 else UP - 1
        for b in range(nb):
            r = src[2 * nt, :, b * LN : (b + 1) * LN].astype(F32)
            for t in range(nt):
                h1[side, b, t, nk - 1 : nk, :] = h1[side, b, t, nk - 1 : nk, :] + r[t : t + 1]
            for t in range(nt):
                f1[b][pl.ds(t * nk * 32 + row, nk, stride=32), :] = h1[side, b, t]

    def step(s, src, k, put):
        ku = jnp.minimum(k + 1, nk - 1)
        kd = jnp.maximum(k - 1, 0)
        for a in range(ni // 8):
            r0 = UP + 8 * a
            c = []
            for f in range(7):
                o = {1: 1, 2: -1}.get(f, 0)
                c.append([co[s, f, b, k, r0 + o : r0 + o + 8, :] for b in range(nb)])
            for t in range(nt):
                x = [src[b, t, k, r0 : r0 + 8, :] for b in range(nb)]
                ns = shifted([x[b] * c[3][b] for b in range(nb)], [x[b] * c[4][b] for b in range(nb)])
                for b in range(nb):
                    y = (x[b] * c[0][b]
                         + src[b, t, k, r0 + 1 : r0 + 9, :] * c[1][b]
                         + src[b, t, k, r0 - 1 : r0 + 7, :] * c[2][b]
                         + ns[b]
                         + src[b, t, ku, r0 : r0 + 8, :] * c[5][b]
                         + src[b, t, kd, r0 : r0 + 8, :] * c[6][b])
                    put(a, b, t, k, y)

    def put1(a, b, t, k, y):
        l1[b, t, k, UP + 8 * a : UP + 8 * a + 8, :] = y

    def body1(k, _):
        step(0, l0, k, put1)
        return 0

    lax.fori_loop(0, nk, body1, 0)

    for t in range(nt):
        r = rows[t].astype(F32)
        for b in range(nb):
            l1[b, t, nk - 1, UP : UP + ni, :] = l1[b, t, nk - 1, UP : UP + ni, :] + r[:, b * LN : (b + 1) * LN]

    def put2(a, b, t, k, y):
        res[t, k, 8 * a : 8 * a + 8, b * LN : (b + 1) * LN] = y

    def body2(k, _):
        step(1, l1, k, put2)

        @pl.when(k == nk - 1)
        def _():
            for t in range(nt):
                res[t, nk - 1] = res[t, nk - 1] + rows[t].astype(F32)

        pltpu.make_async_copy(res.at[:, k], out.at[:, k], osem).start()
        return 0

    lax.fori_loop(0, nk, body2, 0)
    pltpu.make_async_copy(res, out, osem).wait()


def main(ids, lam, met, edges, from_w, from_e, forcing):
    nt, nk, ni, nj = lam.shape
    nb = nj // LN
    return pl.pallas_call(
        main_kernel,
        out_shape=jax.ShapeDtypeStruct(lam.shape, F32),
        in_specs=[SM, HB, VM, VM, VM, VM, HB],
        out_specs=HB,
        scratch_shapes=[
            pltpu.VMEM((nb, nt, nk, 32, LN), F32),
            pltpu.VMEM((nb, nt, nk, 32, LN), F32),
            pltpu.VMEM((2, 7, nb, nk, 32, LN), F32),
            pltpu.VMEM((4, nb, nt, nk, LN), F32),
            pltpu.VMEM((2, 7, nb, nk, LN), F32),
            pltpu.VMEM((2, nb, nt, nk, LN), F32),
            pltpu.VMEM((nt, ni, nj), BF),
            pltpu.VMEM((nt, nk, ni, nj), F32),
            pltpu.SemaphoreType.DMA((nb,)),
            pltpu.SemaphoreType.DMA((nt,)),
            pltpu.SemaphoreType.DMA,
        ],
        compiler_params=pltpu.CompilerParams(vmem_limit_bytes=60 * 1024 * 1024),
        name="steps",
    )(ids, lam, met, edges, from_w, from_e, forcing)


def per_device(adjoint_state, met_fields, forcing, cluster_ids, hour_index):
    own, edge_w, edge_e = pick(hour_index, met_fields)
    got_e = passed_along(edge_w, "tile", -1)
    got_w = passed_along(edge_e, "tile", 1)
    to_w, to_e = pack(cluster_ids, adjoint_state, forcing)
    from_e = passed_along(to_w, "tile", -1)
    from_w = passed_along(to_e, "tile", 1)
    met = lax.all_gather(own, "rcpt", axis=0)
    edges = lax.all_gather(jnp.stack([got_e, got_w]), "rcpt", axis=0)
    return main(cluster_ids, adjoint_state, met, edges, from_w, from_e, forcing)


def solution(mesh):
    placed = (
        P("rcpt", None, "tile", None),
        P(None, None, "rcpt", "tile", None),
        P(None, "tile", None),
        P("rcpt"),
        P(),
    )
    return jax.shard_map(
        per_device,
        mesh=mesh,
        in_specs=placed,
        out_specs=P("rcpt", None, "tile", None),
        check_vma=False,
    )
```

```python
import jax
import jax.numpy as jnp
from jax import lax
from jax.experimental import pallas as pl
from jax.experimental.pallas import tpu as pltpu
from jax.sharding import PartitionSpec as P


BF = jnp.bfloat16
F32 = jnp.float32
SM = pl.BlockSpec(memory_space=pltpu.SMEM)
VM = pl.BlockSpec(memory_space=pltpu.VMEM)
HB = pl.BlockSpec(memory_space=pltpu.HBM)
LN = 128
UP = 8
GR = 40
KP = 17
UN = 2
MIB = 1024 * 1024
DMA = pltpu.SemaphoreType.DMA


def passed_along(block, axis, distance):
    n = lax.axis_size(axis)
    return lax.ppermute(block, axis, [((i - distance) % n, i) for i in range(n)])


def swapped(block, axis, bit):
    return lax.ppermute(block, axis, [(i ^ bit, i) for i in range(lax.axis_size(axis))])


def pack_kernel(hour, ids, lam, met, forcing, own, to_w, to_e, edge_w, edge_e, l0, l1, rows, hs, js, sem, rsem, msem, isem):
    nt, nk, ni, nj = lam.shape
    nb = nj // LN
    ch = 2
    small = [pltpu.make_async_copy(hour, hs, isem.at[0]), pltpu.make_async_copy(ids, js, isem.at[1])]
    copies = [
        [
            pltpu.make_async_copy(
                lam.at[ch * t : ch * t + ch, :, :, b * LN : (b + 1) * LN],
                l0.at[b, ch * t : ch * t + ch, 0:nk, UP : UP + ni, :],
                sem.at[t, b],
            )
            for b in range(nb)
        ]
        for t in range(nt // ch)
    ]
    for c in small + copies[0] + copies[1]:
        c.start()
    for c in small:
        c.wait()
    mcopies = [pltpu.make_async_copy(met.at[hs[s]], own.at[s], msem.at[s]) for s in range(2)]
    rcopies = [pltpu.make_async_copy(forcing.at[js[t]], rows.at[t], rsem.at[t]) for t in range(nt)]
    for c in mcopies + rcopies:
        c.start()
    for cs in copies[2:]:
        for c in cs:
            c.start()
    zero = jnp.zeros((8, LN), F32)

    def clear(t, _):
        for b in range(nb):
            for k in range(nk):
                for ref in (l0, l1):
                    ref[b, t, k, UP - 8 : UP, :] = zero
                    ref[b, t, k, UP + ni : UP + ni + 8, :] = zero
        return 0

    lax.fori_loop(0, nt, clear, 0)
    for c in mcopies:
        c.wait()
    for out, lo, near, far in ((edge_w, 0, 0, 1), (edge_e, ni - 8, ni - 1, ni - 2)):
        for s, f, outs in ((0, 0, ((0, near), (4, far))), (0, 1, ((1, near),)),
                           (0, 2, ((2, near),)), (1, 0, ((3, near),))):
            x = [own[s, f, q, lo : lo + 8, :].astype(F32) for q in range(own.shape[2])]
            for n, c in outs:
                out[n] = jnp.concatenate([y[c - lo : c - lo + 1] for y in x], axis=0).astype(BF)
    for cs, t0 in zip(copies, range(0, nt, ch)):
        for b in range(nb):
            cs[b].wait()
            flat = l0.at[b].reshape(nt * KP * GR, LN)
            for t in range(t0, t0 + ch):
                for out, near, far in ((to_w, 0, 1), (to_e, ni - 1, ni - 2)):
                    for n, c in enumerate((near, far)):
                        x = flat[pl.ds(t * KP * GR + UP + c, nk, stride=GR), :]
                        out[n * nt + t, :, b * LN : (b + 1) * LN] = x.astype(BF)
    for c in rcopies:
        c.wait()
    for t in range(nt):
        r = rows[t].astype(F32)
        to_w[2 * nt, t] = r[0].astype(BF)
        to_e[2 * nt, t] = r[ni - 1].astype(BF)


def pack(hour, ids, lam, met, forcing):
    nt, nk, ni, nj = lam.shape
    nb = nj // LN
    out = jax.ShapeDtypeStruct((2 * nt + 1, nk, nj), BF)
    edge = jax.ShapeDtypeStruct((5, met.shape[2], nj), BF)
    return pl.pallas_call(
        pack_kernel,
        out_shape=[
            jax.ShapeDtypeStruct((2,) + met.shape[1:], BF),
            out,
            out,
            edge,
            edge,
            pltpu.VMEM((nb, nt, KP, GR, LN), F32),
            pltpu.VMEM((nb, nt, KP, GR, LN), F32),
            pltpu.VMEM((nt, ni, nj), BF),
        ],
        in_specs=[HB] * 5,
        out_specs=[VM] * 8,
        scratch_shapes=[
            pltpu.SMEM((2,), jnp.int32), pltpu.SMEM((nt,), jnp.int32),
            DMA((nt // 2, nb)), DMA((nt,)), DMA((2,)), DMA((2,)),
        ],
        compiler_params=pltpu.CompilerParams(vmem_limit_bytes=4 * MIB),
        cost_estimate=pl.CostEstimate(flops=10**6, bytes_accessed=10 * MIB, transcendentals=0),
        name="pack",
    )(hour, ids, lam, met, forcing)


def roll2(x, sh):
    return pltpu.roll(x, sh % LN, 1)


def ends():
    lane = lax.broadcasted_iota(jnp.int32, (8, LN), 1)
    return lane == 0, lane == LN - 1


def shifted(p, o):
    first, last = ends()
    nb = len(p)
    rp = [roll2(x, -1) for x in p]
    ro = [roll2(x, 1) for x in o]
    return [jnp.where(last, rp[(b + 1) % nb], rp[b]) + jnp.where(first, ro[(b - 1) % nb], ro[b]) for b in range(nb)]


def steps_kernel(m0, m1, m2, m3, l0, l1in, rows, res, oc, l1, co, kz):
    ms = (m0, m1, m2, m3)
    _, _, nl, ni, nj = m0.shape
    nb = nj // LN
    nt = rows.shape[0]
    nk = nl * len(ms)
    na = ni // 8
    r = lax.axis_index("rcpt")
    first, last = ends()
    zero = jnp.zeros((8, LN), F32)

    for s in range(2):
        for b in range(nb):
            for a in range(na):
                kz[s, b, 0, 8 * a : 8 * a + 8, :] = zero
            for k in range(nk):
                co[s, 1, b, k, UP + ni : UP + ni + 8, :] = zero
                co[s, 2, b, k, 0:UP, :] = zero
    for m, ref in enumerate(ms):
        base = (r ^ m) * nl

        def coeffs(q, _):
            k = base + q
            top = jnp.where(k < nk - 1, 1.0, 0.0).astype(F32)
            for s in range(2):
                for b in range(nb):
                    for a in range(na):
                        i = 8 * a
                        cx, cy, mx = (ref[s, f, q, i : i + 8, b * LN : (b + 1) * LN].astype(F32) for f in range(3))
                        n = jnp.maximum(cy, 0.0)
                        o = n - cy
                        e = jnp.maximum(cx, 0.0)
                        w = e - cx
                        co[s, 0, b, k, UP + i : UP + i + 8, :] = 1.0 - jnp.abs(cx) - jnp.abs(cy)
                        co[s, 1, b, k, UP + i : UP + i + 8, :] = e
                        co[s, 2, b, k, UP + i : UP + i + 8, :] = w
                        co[s, 3, b, k, UP + i : UP + i + 8, :] = jnp.where(first, 0.0, n) if b == 0 else n
                        co[s, 4, b, k, UP + i : UP + i + 8, :] = jnp.where(last, 0.0, o) if b == nb - 1 else o
                        kz[s, b, k + 1, i : i + 8, :] = (0.02 + 0.25 * jnp.abs(mx)) * top
            return 0

        lax.fori_loop(0, nl, coeffs, 0)

    def run(s, src, put):
        def one(k):
            ku = jnp.minimum(k + 1, nk - 1)
            kd = jnp.maximum(k - 1, 0)
            for a in range(na):
                r0 = UP + 8 * a
                c = []
                for b in range(nb):
                    up = kz[s, b, k + 1, 8 * a : 8 * a + 8, :]
                    dn = kz[s, b, k, 8 * a : 8 * a + 8, :]
                    ce = co[s, 0, b, k, r0 : r0 + 8, :] - up - dn
                    c.append((ce, co[s, 1, b, k, r0 + 1 : r0 + 9, :], co[s, 2, b, k, r0 - 1 : r0 + 7, :], up, dn,
                     co[s, 3, b, k, r0 : r0 + 8, :], co[s, 4, b, k, r0 : r0 + 8, :]))
                for t in range(nt):
                    x = [src[b, t, k, r0 : r0 + 8, :] for b in range(nb)]
                    y = shifted([x[b] * c[b][5] for b in range(nb)], [x[b] * c[b][6] for b in range(nb)])
                    for b in range(nb):
                        ce, ea, we, up, dn, _, _ = c[b]
                        z = ((x[b] * ce + src[b, t, k, r0 + 1 : r0 + 9, :] * ea)
                         + (src[b, t, k, r0 - 1 : r0 + 7, :] * we
                         + src[b, t, ku, r0 : r0 + 8, :] * up)
                         + src[b, t, kd, r0 : r0 + 8, :] * dn) + y[b]
                        put(a, b, t, k, z)

        def body(k, _):
            for u in range(UN):
                one(UN * k + u)
            return 0

        lax.fori_loop(0, nk // UN, body, 0)

    def put1(a, b, t, k, y):
        l1[b, t, k, UP + 8 * a : UP + 8 * a + 8, :] = y

    run(0, l0, put1)
    for t in range(nt):
        x = rows[t].astype(F32)
        for b in range(nb):
            l1[b, t, nk - 1, UP : UP + ni, :] = l1[b, t, nk - 1, UP : UP + ni, :] + x[:, b * LN : (b + 1) * LN]

    def put2(a, b, t, k, y):
        res[b, t, k, 8 * a : 8 * a + 8, :] = y

    run(1, l1, put2)
    for t in range(nt):
        x = rows[t].astype(F32)
        for b in range(nb):
            res[b, t, nk - 1] = res[b, t, nk - 1] + x[:, b * LN : (b + 1) * LN]

    for side, c, out in ((0, ni - 1, 2), (1, 0, 1)):
        for b in range(nb):
            def take(s, f):
                return co.at[s, f, b].reshape(nk * GR, LN)[pl.ds(UP + c, nk, stride=GR), :]

            def mix(d):
                return kz.at[1, b].reshape((nk + 1) * ni, LN)[pl.ds(d * ni + c, nk, stride=ni), :]

            oc[side, 0, b] = take(0, out)
            up, dn = mix(1), mix(0)
            oc[side, 1, b] = take(1, 0) - up - dn
            oc[side, 2, b] = take(1, 2 - side - (1 if side == 0 else -1))
            oc[side, 3, b] = take(1, 3)
            oc[side, 4, b] = take(1, 4)
            oc[side, 5, b] = up
            oc[side, 6, b] = dn


def steps(ms, l0, l1, rows):
    _, _, nl, ni, _ = ms[0].shape
    nb, nt = l0.shape[:2]
    nk = nl * len(ms)
    return pl.pallas_call(
        steps_kernel,
        out_shape=[
            pltpu.VMEM((nb, nt, KP, ni, LN), F32),
            pltpu.VMEM((2, 7, nb, nk, LN), F32),
            pltpu.VMEM(l1.shape, F32),
        ],
        in_specs=[VM] * 7,
        out_specs=[VM] * 3,
        input_output_aliases={5: 2},
        scratch_shapes=[
            pltpu.VMEM((2, 5, nb, nk, GR, LN), F32),
            pltpu.VMEM((2, nb, nk + 1, ni, LN), F32),
        ],
        compiler_params=pltpu.CompilerParams(
            vmem_limit_bytes=12 * MIB),
        cost_estimate=pl.CostEstimate(flops=4 * 10**7, bytes_accessed=20 * MIB, transcendentals=0),
        name="steps",
    )(*ms, l0, l1, rows)[:2]


def finish_kernel(res, l0, oc, from_w, from_e, e0, e1, e2, e3, out, hs, hc, rh, et, osem):
    nb, nt, _, ni, _ = res.shape
    nk = oc.shape[3]
    lanes = lax.broadcasted_iota(jnp.int32, (nk, LN), 1)
    levs = lax.broadcasted_iota(jnp.int32, (nk, LN), 0)
    zero = jnp.zeros((8, LN), F32)
    r = lax.axis_index("rcpt")
    nl = nk // 4
    for m, ref in enumerate((e0, e1, e2, e3)):
        for side in range(2):
            for n in range(5):
                x = ref[side, n].astype(F32)
                for q in range(nl):
                    et[side, n, pl.ds((r ^ m) * nl + q, 1), :] = x[q : q + 1]
    for side, src in ((0, from_e), (1, from_w)):
        sg = 1.0 if side == 0 else -1.0
        for b in range(nb):
            sl = slice(b * LN, (b + 1) * LN)
            hs[side, b, 0:8, :] = zero
            hs[side, b, 8 + nt * nk : 16 + nt * nk, :] = zero
            for t in range(nt):
                hs[side, b, 8 + t * nk : 8 + t * nk + nk, :] = src[t, :, sl].astype(F32)
                rh[side, b, 8 * t : 8 * t + 8, :] = zero
            x = src[2 * nt, :, sl].astype(F32)
            for t in range(nt):
                rh[side, b, 8 * t + 7 : 8 * t + 8, :] = x[t : t + 1]
            cx, cy, m, cx1, far = (et[side, n, :, sl] for n in range(5))
            kk = 0.02 + 0.25 * jnp.abs(m)
            ku = jnp.where(levs == nk - 1, 0.0, kk)
            km = jnp.where(levs == 0, 0.0, pltpu.roll(kk, 1, 0))
            n = jnp.maximum(cy, 0.0)
            o = n - cy
            hc[side, 0, b, 0:nk] = 1.0 - jnp.abs(cx) - jnp.abs(cy) - ku - km
            hc[side, 1, b, 0:nk] = jnp.maximum(sg * far, 0.0)
            hc[side, 2, b, 0:nk] = oc[side, 0, b]
            hc[side, 3, b, 0:nk] = jnp.where(lanes == 0, 0.0, n) if b == 0 else n
            hc[side, 4, b, 0:nk] = jnp.where(lanes == LN - 1, 0.0, o) if b == nb - 1 else o
            hc[side, 5, b, 0:nk] = ku
            hc[side, 6, b, 0:nk] = km
            hc[side, 7, b, 0:8] = zero
            hc[side, 7, b, 8 : 8 + nk] = jnp.maximum(sg * cx, 0.0)
            hc[side, 7, b, 8 + nk : 16 + nk] = zero
            hc[side, 8, b, 0:nk] = jnp.maximum(sg * cx1, 0.0)
    fr = [res.at[b].reshape(nt * KP * ni, LN) for b in range(nb)]
    f0 = [l0.at[b].reshape(nt * KP * GR, LN) for b in range(nb)]

    def one(t, _):
        for side, own, inner in ((0, ni - 1, ni - 2), (1, 0, 1)):
            for h in range(nk // 8):
                k0 = 8 * h
                c = [[hc[side, f, b, k0 : k0 + 8, :] for b in range(nb)] for f in range(7)]
                p = [[oc[side, f, b, k0 : k0 + 8, :] for b in range(nb)] for f in range(7)]
                e = [[hc[side, 7, b, 8 + k0 + d : 16 + k0 + d, :] for b in range(nb)] for d in (-1, 0, 1)]
                ez = [hc[side, 8, b, k0 : k0 + 8, :] for b in range(nb)]
                g = (from_e, from_w)[side]
                x = [[hs[side, b, pl.ds(8 + t * nk + k0 + d, 8), :] for b in range(nb)] for d in (-1, 0, 1)]
                dl = [[x[d][b] * e[d][b] for b in range(nb)] for d in range(3)]
                far = [g[nt + t, k0 : k0 + 8, b * LN : (b + 1) * LN].astype(F32) for b in range(nb)]
                mine = [f0[b][pl.ds((t * KP + k0) * GR + UP + own, 8, stride=GR), :] for b in range(nb)]
                sh = shifted([x[1][b] * c[3][b] for b in range(nb)], [x[1][b] * c[4][b] for b in range(nb)])
                sd = shifted([dl[1][b] * p[3][b] for b in range(nb)], [dl[1][b] * p[4][b] for b in range(nb)])
                for b in range(nb):
                    y = (x[1][b] * c[0][b] + far[b] * c[1][b] + mine[b] * c[2][b] + sh[b]
                         + x[2][b] * c[5][b] + x[0][b] * c[6][b])
                    if h == nk // 8 - 1:
                        y = y + rh[side, b, pl.ds(8 * t, 8), :]
                    z = (y * ez[b] + dl[1][b] * p[1][b] + sd[b]
                         + dl[2][b] * p[5][b] + dl[0][b] * p[6][b])
                    at = pl.ds((t * KP + k0) * ni + own, 8, stride=ni)
                    fr[b][at, :] = fr[b][at, :] + z
                    at = pl.ds((t * KP + k0) * ni + inner, 8, stride=ni)
                    fr[b][at, :] = fr[b][at, :] + dl[1][b] * p[2][b]
        for b in range(nb):
            pltpu.make_async_copy(res.at[b, t, 0:nk], out.at[t, :, :, b * LN : (b + 1) * LN], osem.at[b]).start()
        return 0

    lax.fori_loop(0, nt, one, 0)
    for b in range(nb):
        pltpu.make_async_copy(res.at[b, :, 0:nk], out.at[:, :, :, b * LN : (b + 1) * LN], osem.at[b]).wait()


def finish(res, l0, oc, from_w, from_e, es):
    nb, nt, _, ni, _ = res.shape
    nk = oc.shape[3]
    return pl.pallas_call(
        finish_kernel,
        out_shape=jax.ShapeDtypeStruct((nt, nk, ni, nb * LN), F32),
        in_specs=[VM] * 9,
        out_specs=HB,
        scratch_shapes=[
            pltpu.VMEM((2, nb, 16 + nt * nk, LN), F32),
            pltpu.VMEM((2, 9, nb, 16 + nk, LN), F32),
            pltpu.VMEM((2, nb, 8 * nt, LN), F32),
            pltpu.VMEM((2, 5, nk, nb * LN), F32),
            DMA((nb,)),
        ],
        compiler_params=pltpu.CompilerParams(vmem_limit_bytes=16 * MIB),
        cost_estimate=pl.CostEstimate(flops=10**6, bytes_accessed=8 * MIB, transcendentals=0),
        name="finish",
    )(res, l0, oc, from_w, from_e, *es)


def one_device(*inputs):
    lam, met, src, ids, hour = (pltpu.with_memory_space_constraint(x, pltpu.HBM) for x in inputs)
    own, to_w, to_e, edge_w, edge_e, l0, l1, rows = pack(hour, ids, lam, met, src)
    g2 = swapped(own, "rcpt", 2)
    got_e = passed_along(edge_w, "tile", -1)
    got_w = passed_along(edge_e, "tile", 1)
    from_e = passed_along(to_w, "tile", -1)
    from_w = passed_along(to_e, "tile", 1)
    g1 = swapped(own, "rcpt", 1)
    g3 = swapped(g2, "rcpt", 1)
    e0 = jnp.stack([got_e, got_w])
    es = [e0] + [swapped(e0, "rcpt", m) for m in (1, 2, 3)]
    res, oc = steps((own, g1, g2, g3), l0, l1, rows)
    return finish(res, l0, oc, from_w, from_e, es)


def solution(mesh):
    placed = (
        P("rcpt", None, "tile", None),
        P(None, None, "rcpt", "tile", None),
        P(None, "tile", None),
        P("rcpt"),
        P(),
    )
    return jax.shard_map(
        one_device,
        mesh=mesh,
        in_specs=placed,
        out_specs=P("rcpt", None, "tile", None),
        check_vma=False,
    )
```

```python
import jax
import jax.numpy as jnp
from jax import lax
from jax.experimental import pallas as pl
from jax.experimental.pallas import tpu as pltpu
from jax.sharding import PartitionSpec as P


BF = jnp.bfloat16
F32 = jnp.float32
SM = pl.BlockSpec(memory_space=pltpu.SMEM)
VM = pl.BlockSpec(memory_space=pltpu.VMEM)
HB = pl.BlockSpec(memory_space=pltpu.HBM)
LN = 128
UP = 8
GR = 40
KP = 17
UN = 8
UF = 4
MIB = 1024 * 1024
DMA = pltpu.SemaphoreType.DMA


def passed_along(block, axis, distance):
    n = lax.axis_size(axis)
    return lax.ppermute(block, axis, [((i - distance) % n, i) for i in range(n)])


def swapped(block, axis, bit):
    return lax.ppermute(block, axis, [(i ^ bit, i) for i in range(lax.axis_size(axis))])


def pack_kernel(hour, ids, lam, met, forcing, own, to_w, to_e, edge_w, edge_e, l0, l1, rows, hs, js, sem, rsem, msem, isem):
    nt, nk, ni, nj = lam.shape
    nb = nj // LN
    ch = 2
    small = [pltpu.make_async_copy(hour, hs, isem.at[0]), pltpu.make_async_copy(ids, js, isem.at[1])]
    copies = [
        [
            pltpu.make_async_copy(
                lam.at[ch * t : ch * t + ch, :, :, b * LN : (b + 1) * LN],
                l0.at[b, ch * t : ch * t + ch, 0:nk, UP : UP + ni, :],
                sem.at[t, b],
            )
            for b in range(nb)
        ]
        for t in range(nt // ch)
    ]
    for c in small:
        c.start()
    for cs in copies:
        for c in cs:
            c.start()
    for c in small:
        c.wait()
    mcopies = [pltpu.make_async_copy(met.at[hs[s]], own.at[s], msem.at[s]) for s in range(2)]
    rcopies = [pltpu.make_async_copy(forcing.at[js[t]], rows.at[t], rsem.at[t]) for t in range(nt)]
    for c in mcopies + rcopies:
        c.start()
    zero = jnp.zeros((8, LN), F32)

    def clear(t, _):
        for b in range(nb):
            for ref in (l0, l1):
                flat = ref.at[b].reshape(nt * KP * GR, LN)
                for row in (UP - 1, UP + ni):
                    for k in range(0, nk, 8):
                        flat[pl.ds((t * KP + k) * GR + row, 8, stride=GR), :] = zero
        return 0

    lax.fori_loop(0, nt, clear, 0)
    for cs, t0 in zip(copies, range(0, nt, ch)):
        for b in range(nb):
            cs[b].wait()
            flat = l0.at[b].reshape(nt * KP * GR, LN)
            for t in range(t0, t0 + ch):
                for out, near, far in ((to_w, 0, 1), (to_e, ni - 1, ni - 2)):
                    for n, c in enumerate((near, far)):
                        x = flat[pl.ds(t * KP * GR + UP + c, nk, stride=GR), :]
                        out[n * nt + t, :, b * LN : (b + 1) * LN] = x.astype(BF)
    for c in rcopies:
        c.wait()
    for t in range(nt):
        r = rows[t].astype(F32)
        to_w[2 * nt, t] = r[0].astype(BF)
        to_e[2 * nt, t] = r[ni - 1].astype(BF)
    for c in mcopies:
        c.wait()
    for out, lo, near, far in ((edge_w, 0, 0, 1), (edge_e, ni - 8, ni - 1, ni - 2)):
        for s, f, outs in ((0, 0, ((0, near), (4, far))), (0, 1, ((1, near),)),
                           (0, 2, ((2, near),)), (1, 0, ((3, near),))):
            x = [own[s, f, q, lo : lo + 8, :].astype(F32) for q in range(own.shape[2])]
            for n, c in outs:
                out[n] = jnp.concatenate([y[c - lo : c - lo + 1] for y in x], axis=0).astype(BF)


def pack(hour, ids, lam, met, forcing):
    nt, nk, ni, nj = lam.shape
    nb = nj // LN
    out = jax.ShapeDtypeStruct((2 * nt + 1, nk, nj), BF)
    edge = jax.ShapeDtypeStruct((5, met.shape[2], nj), BF)
    return pl.pallas_call(
        pack_kernel,
        out_shape=[
            jax.ShapeDtypeStruct((2,) + met.shape[1:], BF),
            out,
            out,
            edge,
            edge,
            pltpu.VMEM((nb, nt, KP, GR, LN), F32),
            pltpu.VMEM((nb, nt, KP, GR, LN), F32),
            pltpu.VMEM((nt, ni, nj), BF),
        ],
        in_specs=[HB] * 5,
        out_specs=[VM] * 8,
        scratch_shapes=[
            pltpu.SMEM((2,), jnp.int32), pltpu.SMEM((nt,), jnp.int32),
            DMA((nt // 2, nb)), DMA((nt,)), DMA((2,)), DMA((2,)),
        ],
        compiler_params=pltpu.CompilerParams(vmem_limit_bytes=4 * MIB),
        cost_estimate=pl.CostEstimate(flops=10**6, bytes_accessed=10 * MIB, transcendentals=0),
        name="pack",
    )(hour, ids, lam, met, forcing)


def roll2(x, sh):
    return pltpu.roll(x, sh % LN, 1)


def ends():
    lane = lax.broadcasted_iota(jnp.int32, (8, LN), 1)
    return lane == 0, lane == LN - 1


def shifted(x, n, o):
    first, last = ends()
    nb = len(x)
    out = []
    for b in range(nb):
        p = jnp.where(first, x[b + 1], x[b]) if b + 1 < nb else x[b]
        q = jnp.where(last, x[b - 1], x[b]) if b else x[b]
        out.append(roll2(p * n[b], -1) + roll2(q * o[b], 1))
    return out


def seam(n, o, first, last):
    nb = len(n)
    return (
        [jnp.where(first, n[b + 1] if b + 1 < nb else 0.0, n[b]) for b in range(nb)],
        [jnp.where(last, o[b - 1] if b else 0.0, o[b]) for b in range(nb)],
    )


def steps_kernel(m0, m1, m2, m3, l0, l1in, rows, res, oc, l1, co, kz):
    ms = (m0, m1, m2, m3)
    _, _, nl, ni, nj = m0.shape
    nb = nj // LN
    nt = rows.shape[0]
    nk = nl * len(ms)
    na = ni // 8
    r = lax.axis_index("rcpt")
    first, last = ends()
    zero = jnp.zeros((8, LN), F32)

    for s in range(2):
        for b in range(nb):
            for a in range(na):
                kz[s, b, 0, 8 * a : 8 * a + 8, :] = zero
            for k in range(nk):
                co[s, 1, b, k, UP + ni : UP + ni + 8, :] = zero
                co[s, 2, b, k, 0:UP, :] = zero
    for m, ref in enumerate(ms):
        base = (r ^ m) * nl

        def coeffs(q, _):
            k = base + q
            top = jnp.where(k < nk - 1, 1.0, 0.0).astype(F32)
            for s in range(2):
                for a in range(na):
                    i = 8 * a
                    ns, os = [], []
                    for b in range(nb):
                        cx, cy, mx = (ref[s, f, q, i : i + 8, b * LN : (b + 1) * LN].astype(F32) for f in range(3))
                        e = jnp.maximum(cx, 0.0)
                        ns.append(jnp.maximum(cy, 0.0))
                        os.append(ns[b] - cy)
                        co[s, 0, b, k, UP + i : UP + i + 8, :] = 1.0 - jnp.abs(cx) - jnp.abs(cy)
                        co[s, 1, b, k, UP + i : UP + i + 8, :] = e
                        co[s, 2, b, k, UP + i : UP + i + 8, :] = e - cx
                        kz[s, b, k + 1, i : i + 8, :] = (0.02 + 0.25 * jnp.abs(mx)) * top
                    ns, os = seam(ns, os, first, last)
                    for b in range(nb):
                        co[s, 3, b, k, UP + i : UP + i + 8, :] = ns[b]
                        co[s, 4, b, k, UP + i : UP + i + 8, :] = os[b]
            return 0

        lax.fori_loop(0, nl, coeffs, 0)

    def run(s, src, put):
        def one(k):
            ku = jnp.minimum(k + 1, nk - 1)
            kd = jnp.maximum(k - 1, 0)
            for a in range(na):
                r0 = UP + 8 * a
                c = []
                for b in range(nb):
                    up = kz[s, b, k + 1, 8 * a : 8 * a + 8, :]
                    dn = kz[s, b, k, 8 * a : 8 * a + 8, :]
                    ce = co[s, 0, b, k, r0 : r0 + 8, :] - up - dn
                    c.append((ce, co[s, 1, b, k, r0 + 1 : r0 + 9, :], co[s, 2, b, k, r0 - 1 : r0 + 7, :], up, dn,
                     co[s, 3, b, k, r0 : r0 + 8, :], co[s, 4, b, k, r0 : r0 + 8, :]))
                for t in range(nt):
                    x = [src[b, t, k, r0 : r0 + 8, :] for b in range(nb)]
                    y = shifted(x, [c[b][5] for b in range(nb)], [c[b][6] for b in range(nb)])
                    for b in range(nb):
                        ce, ea, we, up, dn, _, _ = c[b]
                        z = ((x[b] * ce + src[b, t, k, r0 + 1 : r0 + 9, :] * ea)
                         + (src[b, t, k, r0 - 1 : r0 + 7, :] * we
                         + src[b, t, ku, r0 : r0 + 8, :] * up)
                         + src[b, t, kd, r0 : r0 + 8, :] * dn) + y[b]
                        put(a, b, t, k, z)

        def body(k, _):
            for u in range(UN):
                one(UN * k + u)
            return 0

        lax.fori_loop(0, nk // UN, body, 0)

    def put1(a, b, t, k, y):
        l1[b, t, k, UP + 8 * a : UP + 8 * a + 8, :] = y

    run(0, l0, put1)
    for t in range(nt):
        x = rows[t].astype(F32)
        for b in range(nb):
            l1[b, t, nk - 1, UP : UP + ni, :] = l1[b, t, nk - 1, UP : UP + ni, :] + x[:, b * LN : (b + 1) * LN]

    def put2(a, b, t, k, y):
        res[b, t, k, 8 * a : 8 * a + 8, :] = y

    run(1, l1, put2)
    for t in range(nt):
        x = rows[t].astype(F32)
        for b in range(nb):
            res[b, t, nk - 1] = res[b, t, nk - 1] + x[:, b * LN : (b + 1) * LN]

    for side, c, out in ((0, ni - 1, 2), (1, 0, 1)):
        for b in range(nb):
            def take(s, f):
                return co.at[s, f, b].reshape(nk * GR, LN)[pl.ds(UP + c, nk, stride=GR), :]

            def mix(d):
                return kz.at[1, b].reshape((nk + 1) * ni, LN)[pl.ds(d * ni + c, nk, stride=ni), :]

            oc[side, 0, b] = take(0, out)
            up, dn = mix(1), mix(0)
            oc[side, 1, b] = take(1, 0) - up - dn
            oc[side, 2, b] = take(1, 2 - side - (1 if side == 0 else -1))
            oc[side, 3, b] = take(1, 3)
            oc[side, 4, b] = take(1, 4)
            oc[side, 5, b] = up
            oc[side, 6, b] = dn


def steps(ms, l0, l1, rows):
    _, _, nl, ni, _ = ms[0].shape
    nb, nt = l0.shape[:2]
    nk = nl * len(ms)
    return pl.pallas_call(
        steps_kernel,
        out_shape=[
            pltpu.VMEM((nb, nt, KP, ni, LN), F32),
            pltpu.VMEM((2, 7, nb, nk, LN), F32),
            pltpu.VMEM(l1.shape, F32),
        ],
        in_specs=[VM] * 7,
        out_specs=[VM] * 3,
        input_output_aliases={5: 2},
        scratch_shapes=[
            pltpu.VMEM((2, 5, nb, nk, GR, LN), F32),
            pltpu.VMEM((2, nb, nk + 1, ni, LN), F32),
        ],
        compiler_params=pltpu.CompilerParams(
            vmem_limit_bytes=12 * MIB),
        cost_estimate=pl.CostEstimate(flops=4 * 10**7, bytes_accessed=20 * MIB, transcendentals=0),
        name="steps",
    )(*ms, l0, l1, rows)[:2]


def finish_kernel(res, l0, oc, from_w, from_e, e0, e1, e2, e3, out, hs, hc, rh, et, osem):
    nb, nt, _, ni, _ = res.shape
    nk = oc.shape[3]
    lanes = lax.broadcasted_iota(jnp.int32, (nk, LN), 1)
    levs = lax.broadcasted_iota(jnp.int32, (nk, LN), 0)
    zero = jnp.zeros((8, LN), F32)
    r = lax.axis_index("rcpt")
    nl = nk // 4
    for m, ref in enumerate((e0, e1, e2, e3)):
        for side in range(2):
            for n in range(5):
                x = ref[side, n].astype(F32)
                for q in range(nl):
                    et[side, n, pl.ds((r ^ m) * nl + q, 1), :] = x[q : q + 1]
    for side, src in ((0, from_e), (1, from_w)):
        sg = 1.0 if side == 0 else -1.0
        ns, os = [], []
        for b in range(nb):
            sl = slice(b * LN, (b + 1) * LN)
            hs[side, b, 0:8, :] = zero
            hs[side, b, 8 + nt * nk : 16 + nt * nk, :] = zero
            for t in range(nt):
                hs[side, b, 8 + t * nk : 8 + t * nk + nk, :] = src[t, :, sl].astype(F32)
                rh[side, b, 8 * t : 8 * t + 8, :] = zero
            x = src[2 * nt, :, sl].astype(F32)
            for t in range(nt):
                rh[side, b, 8 * t + 7 : 8 * t + 8, :] = x[t : t + 1]
            cx, cy, m, cx1, far = (et[side, n, :, sl] for n in range(5))
            kk = 0.02 + 0.25 * jnp.abs(m)
            ku = jnp.where(levs == nk - 1, 0.0, kk)
            km = jnp.where(levs == 0, 0.0, pltpu.roll(kk, 1, 0))
            n = jnp.maximum(cy, 0.0)
            o = n - cy
            hc[side, 0, b, 0:nk] = 1.0 - jnp.abs(cx) - jnp.abs(cy) - ku - km
            hc[side, 1, b, 0:nk] = jnp.maximum(sg * far, 0.0)
            hc[side, 2, b, 0:nk] = oc[side, 0, b]
            ns.append(n)
            os.append(o)
            hc[side, 5, b, 0:nk] = ku
            hc[side, 6, b, 0:nk] = km
            hc[side, 7, b, 0:8] = zero
            hc[side, 7, b, 8 : 8 + nk] = jnp.maximum(sg * cx, 0.0)
            hc[side, 7, b, 8 + nk : 16 + nk] = zero
            hc[side, 8, b, 0:nk] = jnp.maximum(sg * cx1, 0.0)
        ns, os = seam(ns, os, lanes == 0, lanes == LN - 1)
        for b in range(nb):
            hc[side, 3, b, 0:nk] = ns[b]
            hc[side, 4, b, 0:nk] = os[b]
    fr = [res.at[b].reshape(nt * KP * ni, LN) for b in range(nb)]
    f0 = [l0.at[b].reshape(nt * KP * GR, LN) for b in range(nb)]

    def one(t):
        for side, own, inner in ((0, ni - 1, ni - 2), (1, 0, 1)):
            for h in range(nk // 8):
                k0 = 8 * h
                c = [[hc[side, f, b, k0 : k0 + 8, :] for b in range(nb)] for f in range(7)]
                p = [[oc[side, f, b, k0 : k0 + 8, :] for b in range(nb)] for f in range(7)]
                e = [[hc[side, 7, b, 8 + k0 + d : 16 + k0 + d, :] for b in range(nb)] for d in (-1, 0, 1)]
                ez = [hc[side, 8, b, k0 : k0 + 8, :] for b in range(nb)]
                g = (from_e, from_w)[side]
                x = [[hs[side, b, pl.ds(8 + t * nk + k0 + d, 8), :] for b in range(nb)] for d in (-1, 0, 1)]
                dl = [[x[d][b] * e[d][b] for b in range(nb)] for d in range(3)]
                far = [g[nt + t, k0 : k0 + 8, b * LN : (b + 1) * LN].astype(F32) for b in range(nb)]
                mine = [f0[b][pl.ds((t * KP + k0) * GR + UP + own, 8, stride=GR), :] for b in range(nb)]
                sh = shifted(x[1], c[3], c[4])
                sd = shifted(dl[1], p[3], p[4])
                for b in range(nb):
                    y = (x[1][b] * c[0][b] + far[b] * c[1][b] + mine[b] * c[2][b] + sh[b]
                         + x[2][b] * c[5][b] + x[0][b] * c[6][b])
                    if h == nk // 8 - 1:
                        y = y + rh[side, b, pl.ds(8 * t, 8), :]
                    z = (y * ez[b] + dl[1][b] * p[1][b] + sd[b]
                         + dl[2][b] * p[5][b] + dl[0][b] * p[6][b])
                    at = pl.ds((t * KP + k0) * ni + own, 8, stride=ni)
                    fr[b][at, :] = fr[b][at, :] + z
                    at = pl.ds((t * KP + k0) * ni + inner, 8, stride=ni)
                    fr[b][at, :] = fr[b][at, :] + dl[1][b] * p[2][b]
        for b in range(nb):
            pltpu.make_async_copy(res.at[b, t, 0:nk], out.at[t, :, :, b * LN : (b + 1) * LN], osem.at[b]).start()

    def body(h, _):
        for u in range(UF):
            one(UF * h + u)
        return 0

    lax.fori_loop(0, nt // UF, body, 0)
    for b in range(nb):
        pltpu.make_async_copy(res.at[b, :, 0:nk], out.at[:, :, :, b * LN : (b + 1) * LN], osem.at[b]).wait()


def finish(res, l0, oc, from_w, from_e, es):
    nb, nt, _, ni, _ = res.shape
    nk = oc.shape[3]
    return pl.pallas_call(
        finish_kernel,
        out_shape=jax.ShapeDtypeStruct((nt, nk, ni, nb * LN), F32),
        in_specs=[VM] * 9,
        out_specs=HB,
        scratch_shapes=[
            pltpu.VMEM((2, nb, 16 + nt * nk, LN), F32),
            pltpu.VMEM((2, 9, nb, 16 + nk, LN), F32),
            pltpu.VMEM((2, nb, 8 * nt, LN), F32),
            pltpu.VMEM((2, 5, nk, nb * LN), F32),
            DMA((nb,)),
        ],
        compiler_params=pltpu.CompilerParams(
            vmem_limit_bytes=12 * MIB),
        cost_estimate=pl.CostEstimate(flops=10**6, bytes_accessed=8 * MIB, transcendentals=0),
        name="finish",
    )(res, l0, oc, from_w, from_e, *es)


def one_device(*inputs):
    lam, met, src, ids, hour = (pltpu.with_memory_space_constraint(x, pltpu.HBM) for x in inputs)
    own, to_w, to_e, edge_w, edge_e, l0, l1, rows = pack(hour, ids, lam, met, src)
    g2 = swapped(own, "rcpt", 2)
    got_e = passed_along(edge_w, "tile", -1)
    got_w = passed_along(edge_e, "tile", 1)
    from_e = passed_along(to_w, "tile", -1)
    from_w = passed_along(to_e, "tile", 1)
    g1 = swapped(own, "rcpt", 1)
    g3 = swapped(g2, "rcpt", 1)
    e0 = jnp.stack([got_e, got_w])
    es = [e0] + [swapped(e0, "rcpt", m) for m in (1, 2, 3)]
    res, oc = steps((own, g1, g2, g3), l0, l1, rows)
    return finish(res, l0, oc, from_w, from_e, es)


def solution(mesh):
    placed = (
        P("rcpt", None, "tile", None),
        P(None, None, "rcpt", "tile", None),
        P(None, "tile", None),
        P("rcpt"),
        P(),
    )
    return jax.shard_map(
        one_device,
        mesh=mesh,
        in_specs=placed,
        out_specs=P("rcpt", None, "tile", None),
        check_vma=False,
    )
```

```python
import jax
import jax.numpy as jnp
from jax import lax
from jax.experimental import pallas as pl
from jax.experimental.pallas import tpu as pltpu
from jax.sharding import PartitionSpec as P


BF = jnp.bfloat16
F32 = jnp.float32
SM = pl.BlockSpec(memory_space=pltpu.SMEM)
VM = pl.BlockSpec(memory_space=pltpu.VMEM)
HB = pl.BlockSpec(memory_space=pltpu.HBM)
LN = 128
UP = 8
GR = 40
KP = 17
UN = 8
UF = 4
UN2 = 4
MIB = 1024 * 1024
DMA = pltpu.SemaphoreType.DMA


def passed_along(block, axis, distance):
    n = lax.axis_size(axis)
    return lax.ppermute(block, axis, [((i - distance) % n, i) for i in range(n)])


def swapped(block, axis, bit):
    return lax.ppermute(block, axis, [(i ^ bit, i) for i in range(lax.axis_size(axis))])


def pack_kernel(hour, ids, lam, met, forcing, own, to_w, to_e, edge_w, edge_e, l0, l1, rows, hs, js, sem, rsem, msem, isem):
    nt, nk, ni, nj = lam.shape
    nb = nj // LN
    ch = 2
    small = [pltpu.make_async_copy(hour, hs, isem.at[0]), pltpu.make_async_copy(ids, js, isem.at[1])]
    copies = [
        [
            pltpu.make_async_copy(
                lam.at[ch * t : ch * t + ch, :, :, b * LN : (b + 1) * LN],
                l0.at[b, ch * t : ch * t + ch, 0:nk, UP : UP + ni, :],
                sem.at[t, b],
            )
            for b in range(nb)
        ]
        for t in range(nt // ch)
    ]
    for c in small:
        c.start()
    for cs in copies:
        for c in cs:
            c.start()
    for c in small:
        c.wait()
    mcopies = [pltpu.make_async_copy(met.at[hs[s]], own.at[s], msem.at[s]) for s in range(2)]
    rcopies = [pltpu.make_async_copy(forcing.at[js[t]], rows.at[t], rsem.at[t]) for t in range(nt)]
    for c in mcopies + rcopies:
        c.start()
    zero = jnp.zeros((8, LN), F32)

    def clear(t, _):
        for b in range(nb):
            for ref in (l0, l1):
                flat = ref.at[b].reshape(nt * KP * GR, LN)
                for row in (UP - 1, UP + ni):
                    for k in range(0, nk, 8):
                        flat[pl.ds((t * KP + k) * GR + row, 8, stride=GR), :] = zero
        return 0

    lax.fori_loop(0, nt, clear, 0)
    for cs, t0 in zip(copies, range(0, nt, ch)):
        for b in range(nb):
            cs[b].wait()
            flat = l0.at[b].reshape(nt * KP * GR, LN)
            for t in range(t0, t0 + ch):
                for out, near, far in ((to_w, 0, 1), (to_e, ni - 1, ni - 2)):
                    for n, c in enumerate((near, far)):
                        x = flat[pl.ds(t * KP * GR + UP + c, nk, stride=GR), :]
                        out[n * nt + t, :, b * LN : (b + 1) * LN] = x.astype(BF)
    for c in rcopies:
        c.wait()
    for t in range(nt):
        r = rows[t].astype(F32)
        to_w[2 * nt, t] = r[0].astype(BF)
        to_e[2 * nt, t] = r[ni - 1].astype(BF)
    for c in mcopies:
        c.wait()
    for out, lo, near, far in ((edge_w, 0, 0, 1), (edge_e, ni - 8, ni - 1, ni - 2)):
        for s, f, outs in ((0, 0, ((0, near), (4, far))), (0, 1, ((1, near),)),
                           (0, 2, ((2, near),)), (1, 0, ((3, near),))):
            x = [own[s, f, q, lo : lo + 8, :].astype(F32) for q in range(own.shape[2])]
            for n, c in outs:
                out[n] = jnp.concatenate([y[c - lo : c - lo + 1] for y in x], axis=0).astype(BF)


def pack(hour, ids, lam, met, forcing):
    nt, nk, ni, nj = lam.shape
    nb = nj // LN
    out = jax.ShapeDtypeStruct((2 * nt + 1, nk, nj), BF)
    edge = jax.ShapeDtypeStruct((5, met.shape[2], nj), BF)
    return pl.pallas_call(
        pack_kernel,
        out_shape=[
            jax.ShapeDtypeStruct((2,) + met.shape[1:], BF),
            out,
            out,
            edge,
            edge,
            pltpu.VMEM((nb, nt, KP, GR, LN), F32),
            pltpu.VMEM((nb, nt, KP, GR, LN), F32),
            pltpu.VMEM((nt, ni, nj), BF),
        ],
        in_specs=[HB] * 5,
        out_specs=[VM] * 8,
        scratch_shapes=[
            pltpu.SMEM((2,), jnp.int32), pltpu.SMEM((nt,), jnp.int32),
            DMA((nt // 2, nb)), DMA((nt,)), DMA((2,)), DMA((2,)),
        ],
        compiler_params=pltpu.CompilerParams(vmem_limit_bytes=4 * MIB),
        cost_estimate=pl.CostEstimate(flops=10**6, bytes_accessed=10 * MIB, transcendentals=0),
        name="pack",
    )(hour, ids, lam, met, forcing)


def roll2(x, sh):
    return pltpu.roll(x, sh % LN, 1)


def ends():
    lane = lax.broadcasted_iota(jnp.int32, (8, LN), 1)
    return lane == 0, lane == LN - 1


def shifted(x, n, o):
    first, last = ends()
    nb = len(x)
    out = []
    for b in range(nb):
        p = jnp.where(first, x[b + 1], x[b]) if b + 1 < nb else x[b]
        q = jnp.where(last, x[b - 1], x[b]) if b else x[b]
        out.append(roll2(p * n[b], -1) + roll2(q * o[b], 1))
    return out


def seam(n, o, first, last):
    nb = len(n)
    return (
        [jnp.where(first, n[b + 1] if b + 1 < nb else 0.0, n[b]) for b in range(nb)],
        [jnp.where(last, o[b - 1] if b else 0.0, o[b]) for b in range(nb)],
    )


def run(s, src, co, kz, put, un, after):
    nb, nt = src.shape[:2]
    nk = co.shape[3]
    ni = kz.shape[3]
    na = ni // 8

    def one(k):
        ku = jnp.minimum(k + 1, nk - 1)
        kd = jnp.maximum(k - 1, 0)
        for a in range(na):
            r0 = UP + 8 * a
            c = []
            for b in range(nb):
                up = kz[s, b, k + 1, 8 * a : 8 * a + 8, :]
                dn = kz[s, b, k, 8 * a : 8 * a + 8, :]
                ce = co[s, 0, b, k, r0 : r0 + 8, :] - up - dn
                c.append((ce, co[s, 1, b, k, r0 + 1 : r0 + 9, :], co[s, 2, b, k, r0 - 1 : r0 + 7, :], up, dn,
                 co[s, 3, b, k, r0 : r0 + 8, :], co[s, 4, b, k, r0 : r0 + 8, :]))
            for t in range(nt):
                x = [src[b, t, k, r0 : r0 + 8, :] for b in range(nb)]
                y = shifted(x, [c[b][5] for b in range(nb)], [c[b][6] for b in range(nb)])
                for b in range(nb):
                    ce, ea, we, up, dn, _, _ = c[b]
                    z = ((x[b] * ce + src[b, t, k, r0 + 1 : r0 + 9, :] * ea)
                     + (src[b, t, k, r0 - 1 : r0 + 7, :] * we
                     + src[b, t, ku, r0 : r0 + 8, :] * up)
                     + src[b, t, kd, r0 : r0 + 8, :] * dn) + y[b]
                    put(a, b, t, k, z)

    def body(k, _):
        for u in range(un):
            one(un * k + u)
        after(k)
        return 0

    lax.fori_loop(0, nk // un, body, 0)


def first_kernel(m0, m1, m2, m3, l0, l1in, rows, l1, co, kz):
    ms = (m0, m1, m2, m3)
    _, _, nl, ni, nj = m0.shape
    nb = nj // LN
    nt = rows.shape[0]
    nk = nl * len(ms)
    na = ni // 8
    r = lax.axis_index("rcpt")
    first, last = ends()
    zero = jnp.zeros((8, LN), F32)

    for s in range(2):
        for b in range(nb):
            for a in range(na):
                kz[s, b, 0, 8 * a : 8 * a + 8, :] = zero
            for k in range(nk):
                co[s, 1, b, k, UP + ni : UP + ni + 8, :] = zero
                co[s, 2, b, k, 0:UP, :] = zero
    for m, ref in enumerate(ms):
        base = (r ^ m) * nl

        def coeffs(q, _):
            k = base + q
            top = jnp.where(k < nk - 1, 1.0, 0.0).astype(F32)
            for s in range(2):
                for a in range(na):
                    i = 8 * a
                    ns, os = [], []
                    for b in range(nb):
                        cx, cy, mx = (ref[s, f, q, i : i + 8, b * LN : (b + 1) * LN].astype(F32) for f in range(3))
                        e = jnp.maximum(cx, 0.0)
                        ns.append(jnp.maximum(cy, 0.0))
                        os.append(ns[b] - cy)
                        co[s, 0, b, k, UP + i : UP + i + 8, :] = 1.0 - jnp.abs(cx) - jnp.abs(cy)
                        co[s, 1, b, k, UP + i : UP + i + 8, :] = e
                        co[s, 2, b, k, UP + i : UP + i + 8, :] = e - cx
                        kz[s, b, k + 1, i : i + 8, :] = (0.02 + 0.25 * jnp.abs(mx)) * top
                    ns, os = seam(ns, os, first, last)
                    for b in range(nb):
                        co[s, 3, b, k, UP + i : UP + i + 8, :] = ns[b]
                        co[s, 4, b, k, UP + i : UP + i + 8, :] = os[b]
            return 0

        lax.fori_loop(0, nl, coeffs, 0)

    def put1(a, b, t, k, y):
        l1[b, t, k, UP + 8 * a : UP + 8 * a + 8, :] = y

    run(0, l0, co, kz, put1, UN, lambda h: None)
    for t in range(nt):
        x = rows[t].astype(F32)
        for b in range(nb):
            l1[b, t, nk - 1, UP : UP + ni, :] = l1[b, t, nk - 1, UP : UP + ni, :] + x[:, b * LN : (b + 1) * LN]


def first_step(ms, l0, l1, rows):
    _, _, nl, ni, _ = ms[0].shape
    nb, _ = l0.shape[:2]
    nk = nl * len(ms)
    return pl.pallas_call(
        first_kernel,
        out_shape=[
            pltpu.VMEM(l1.shape, F32),
            pltpu.VMEM((2, 5, nb, nk, GR, LN), F32),
            pltpu.VMEM((2, nb, nk + 1, ni, LN), F32),
        ],
        in_specs=[VM] * 7,
        out_specs=[VM] * 3,
        input_output_aliases={5: 0},
        compiler_params=pltpu.CompilerParams(
            vmem_limit_bytes=4 * MIB),
        cost_estimate=pl.CostEstimate(flops=2 * 10**7, bytes_accessed=10 * MIB, transcendentals=0),
        name="first",
    )(*ms, l0, l1, rows)


def second_kernel(l0, l1in, coin, kz, rows, from_w, from_e, e0, e1, e2, e3, out, l1, co, res, hs, hc, rh, et, osem):
    nb, nt, _, ni, _ = res.shape
    nk = co.shape[3]
    lanes = lax.broadcasted_iota(jnp.int32, (nk, LN), 1)
    levs = lax.broadcasted_iota(jnp.int32, (nk, LN), 0)
    zero = jnp.zeros((8, LN), F32)
    r = lax.axis_index("rcpt")
    nl = nk // 4
    for m, ref in enumerate((e0, e1, e2, e3)):
        for side in range(2):
            for n in range(5):
                x = ref[side, n].astype(F32)
                for q in range(nl):
                    et[side, n, pl.ds((r ^ m) * nl + q, 1), :] = x[q : q + 1]
    for side, src in ((0, from_e), (1, from_w)):
        sg = 1.0 if side == 0 else -1.0
        ns, os = [], []
        for b in range(nb):
            sl = slice(b * LN, (b + 1) * LN)
            hs[side, b, 0:8, :] = zero
            hs[side, b, 8 + nt * nk : 16 + nt * nk, :] = zero
            for t in range(nt):
                hs[side, b, 8 + t * nk : 8 + t * nk + nk, :] = src[t, :, sl].astype(F32)
                rh[side, b, 8 * t : 8 * t + 8, :] = zero
            x = src[2 * nt, :, sl].astype(F32)
            for t in range(nt):
                rh[side, b, 8 * t + 7 : 8 * t + 8, :] = x[t : t + 1]
            cx, cy, m, cx1, far = (et[side, n, :, sl] for n in range(5))
            kk = 0.02 + 0.25 * jnp.abs(m)
            ku = jnp.where(levs == nk - 1, 0.0, kk)
            km = jnp.where(levs == 0, 0.0, pltpu.roll(kk, 1, 0))
            n = jnp.maximum(cy, 0.0)
            o = n - cy
            hc[side, 0, b, 0:nk] = 1.0 - jnp.abs(cx) - jnp.abs(cy) - ku - km
            hc[side, 1, b, 0:nk] = jnp.maximum(sg * far, 0.0)
            own, pad, out_f = (UP + ni - 1, UP + ni, 2) if side == 0 else (UP, UP - 1, 1)
            hc[side, 2, b, 0:nk] = co.at[0, out_f, b].reshape(nk * GR, LN)[pl.ds(own, nk, stride=GR), :]
            ns.append(n)
            os.append(o)
            hc[side, 5, b, 0:nk] = ku
            hc[side, 6, b, 0:nk] = km
            hc[side, 7, b, 0:nk] = jnp.maximum(sg * cx, 0.0)
            co.at[1, 1 + side, b].reshape(nk * GR, LN)[pl.ds(pad, nk, stride=GR), :] = jnp.maximum(sg * cx1, 0.0)
        ns, os = seam(ns, os, lanes == 0, lanes == LN - 1)
        for b in range(nb):
            hc[side, 3, b, 0:nk] = ns[b]
            hc[side, 4, b, 0:nk] = os[b]
    f0 = [l0.at[b].reshape(nt * KP * GR, LN) for b in range(nb)]
    f1 = [l1.at[b].reshape(nt * KP * GR, LN) for b in range(nb)]

    def one(t):
        for side, own, pad in ((0, UP + ni - 1, UP + ni), (1, UP, UP - 1)):
            for h in range(nk // 8):
                k0 = 8 * h
                c = [[hc[side, f, b, k0 : k0 + 8, :] for b in range(nb)] for f in range(8)]
                g = (from_e, from_w)[side]
                x = [[hs[side, b, pl.ds(8 + t * nk + k0 + d, 8), :] for b in range(nb)] for d in (-1, 0, 1)]
                far = [g[nt + t, k0 : k0 + 8, b * LN : (b + 1) * LN].astype(F32) for b in range(nb)]
                mine = [f0[b][pl.ds((t * KP + k0) * GR + own, 8, stride=GR), :] for b in range(nb)]
                sh = shifted(x[1], c[3], c[4])
                for b in range(nb):
                    y = (x[1][b] * c[0][b] + far[b] * c[1][b] + mine[b] * c[2][b] + sh[b]
                         + x[2][b] * c[5][b] + x[0][b] * c[6][b])
                    if h == nk // 8 - 1:
                        y = y + rh[side, b, pl.ds(8 * t, 8), :]
                    f1[b][pl.ds((t * KP + k0) * GR + pad, 8, stride=GR), :] = y
                    at = pl.ds((t * KP + k0) * GR + own, 8, stride=GR)
                    f1[b][at, :] = f1[b][at, :] + x[1][b] * c[7][b]

    def outer(h, _):
        for u in range(UF):
            one(UF * h + u)
        return 0

    lax.fori_loop(0, nt // UF, outer, 0)

    def put2(a, b, t, k, y):
        res[b, t, k, 8 * a : 8 * a + 8, :] = y

    def after(h):
        @pl.when(h == nk // UN2 - 1)
        def _():
            for t in range(nt):
                x = rows[t].astype(F32)
                for b in range(nb):
                    res[b, t, nk - 1] = res[b, t, nk - 1] + x[:, b * LN : (b + 1) * LN]

        at = pl.ds(UN2 * h, UN2)
        for b in range(nb):
            pltpu.make_async_copy(res.at[b, :, at], out.at[:, at, :, b * LN : (b + 1) * LN], osem.at[b]).start()

    run(1, l1, co, kz, put2, UN2, after)
    for b in range(nb):
        pltpu.make_async_copy(res.at[b, :, 0:nk], out.at[:, :, :, b * LN : (b + 1) * LN], osem.at[b]).wait()


def second_step(l0, l1, co, kz, rows, from_w, from_e, es):
    nb, nt = l0.shape[:2]
    nk = co.shape[3]
    ni = kz.shape[3]
    return pl.pallas_call(
        second_kernel,
        out_shape=[
            jax.ShapeDtypeStruct((nt, nk, ni, nb * LN), F32),
            pltpu.VMEM(l1.shape, F32),
            pltpu.VMEM(co.shape, F32),
        ],
        in_specs=[VM] * 11,
        out_specs=[HB, VM, VM],
        input_output_aliases={1: 1, 2: 2},
        scratch_shapes=[
            pltpu.VMEM((nb, nt, KP, ni, LN), F32),
            pltpu.VMEM((2, nb, 16 + nt * nk, LN), F32),
            pltpu.VMEM((2, 8, nb, nk, LN), F32),
            pltpu.VMEM((2, nb, 8 * nt, LN), F32),
            pltpu.VMEM((2, 5, nk, nb * LN), F32),
            DMA((nb,)),
        ],
        compiler_params=pltpu.CompilerParams(
            vmem_limit_bytes=12 * MIB),
        cost_estimate=pl.CostEstimate(flops=2 * 10**7, bytes_accessed=14 * MIB, transcendentals=0),
        name="second",
    )(l0, l1, co, kz, rows, from_w, from_e, *es)[0]


def one_device(*inputs):
    lam, met, src, ids, hour = (pltpu.with_memory_space_constraint(x, pltpu.HBM) for x in inputs)
    own, to_w, to_e, edge_w, edge_e, l0, l1, rows = pack(hour, ids, lam, met, src)
    g2 = swapped(own, "rcpt", 2)
    got_e = passed_along(edge_w, "tile", -1)
    got_w = passed_along(edge_e, "tile", 1)
    from_e = passed_along(to_w, "tile", -1)
    from_w = passed_along(to_e, "tile", 1)
    g1 = swapped(own, "rcpt", 1)
    g3 = swapped(g2, "rcpt", 1)
    e0 = jnp.stack([got_e, got_w])
    es = [e0] + [swapped(e0, "rcpt", m) for m in (1, 2, 3)]
    l1, co, kz = first_step((own, g1, g2, g3), l0, l1, rows)
    return second_step(l0, l1, co, kz, rows, from_w, from_e, es)


def solution(mesh):
    placed = (
        P("rcpt", None, "tile", None),
        P(None, None, "rcpt", "tile", None),
        P(None, "tile", None),
        P("rcpt"),
        P(),
    )
    return jax.shard_map(
        one_device,
        mesh=mesh,
        in_specs=placed,
        out_specs=P("rcpt", None, "tile", None),
        check_vma=False,
    )
```
